768 devices in a mesh: dp: 128 (over x, y, z_hi), tensor: 6 (over z_lo, core).
Axes of the slice: x: 4, y: 8, z: 12 (z_hi: 4, z_lo: 3; z = z_hi * 3 + z_lo), core: 2. Of those that a mesh axis runs over, the one named last changes fastest.
Arguments:
- hidden: bfloat16 [18432, 4096], P(('dp', 'tensor')), may hold values from -6 to 6
- doc_ids: int32 [128, 144], replicated, may hold values from 0 to 3, never falling along the last dimension, each value on 1 to 72 neighbouring positions
- teacher: bfloat16 [18432, 8448], P('dp', 'tensor'), may hold values from -6 to 6
- rotation: int32 [1], replicated, may hold values from 0 to 127
- norm_gain_vector: float32 [4096], replicated, may hold values from 0.5 to 1.5
- proj_bias: float32 [8448], P('tensor'), may hold values from -3 to 3
- projection: bfloat16 [4096, 8448], P(None, 'tensor'), may hold values from -0.09375 to 0.09375
Outputs:
- hidden_gradient: bfloat16 [18432, 4096], P(('dp', 'tensor'))
- gain_gradient_mean: float32 [4096], replicated
- grad_bias: float32 [8448], P('tensor')
- distill_loss: float32 [], replicated
The draws below stay inside these ranges and needn't reach their ends.
Inputs may be any that keep to these rules, and one draw needn't show every extreme that they name: `doc_ids`: in each row the document numbers never fall; each document has 1 to 72 tokens and one has exactly 72.
All inputs are finite; a program needn't handle non-finite values.
Results may differ from the reference program's by a relative error of at most 0.0049.
The reference program's roundings to bfloat16 on the way count: a program that leaves them out, or rounds other values in their place, can miss the bound.
Values may be sent and summed in bfloat16 or wider, within the bound.
No kernel may reach another device: no remote copies, remote signals or barrier semaphores. Data moves between devices by JAX's collectives and lax.ppermute only.
A program may use at most 64 MiB of HBM per device.

```python
import math
import jax
import jax.numpy as jnp
import numpy as np
from jax import lax

D = 4096
P_SIZE = 8448
TOK_DEV = 144
DOCS = 4
MOST_DOC = 72
TOKEN_TOTAL = 18432
N_DP = 128


def block_levels(own_key, shape, split, smallest, top_value):
    loudness, own = 1.0, jax.random.fold_in(own_key, 6)
    for axis_at, shards_of in split:
        heights = jnp.exp(jax.random.uniform(jax.random.fold_in(own, axis_at), (shards_of,), jnp.float32, smallest / len(split), top_value / len(split)))
        loudness = loudness * jnp.repeat(heights, shape[axis_at] // shards_of).reshape([-1 if axis == axis_at else 1 for axis in range(len(shape))])
    return loudness


def profile(amount, total, reach, lean):
    portions = [(1 << 20) // math.isqrt(rank ** lean) + 1 for rank in range(2, amount + 1)]
    surplus, holding = total - reach - (amount - 1), [1] * (amount - 1)
    while surplus > 0:
        movable = [i for i in range(amount - 1) if holding[i] < reach]
        whole, budget = sum([portions[i] for i in movable]), surplus
        for i in movable:
            more = min(reach - holding[i], max(1, budget * portions[i] // whole), surplus)
            holding[i] = holding[i] + more
            surplus = surplus - more
    return np.array([reach] + holding)


def uneven_parts(rng, number_of, total, most, slope):
    if number_of == 2:
        one = jax.random.randint(rng, (), max(1, total - most), min(most, total - 1) + 1)
        return jnp.stack([one, total - one])
    sizes = jnp.asarray(profile(number_of, total, most, slope), jnp.int32)
    pairs = (number_of - 1) // 2
    source_of, taker = sizes[1:1 + 2 * pairs:2], sizes[2:2 + 2 * pairs:2]
    margin = jnp.minimum(source_of - 1, most - taker)
    moved = jax.random.randint(jax.random.fold_in(rng, 1), (pairs,), 0, 1 << 20) % (margin + 1)
    sizes = sizes.at[1:1 + 2 * pairs:2].set(source_of - moved).at[2:2 + 2 * pairs:2].set(taker + moved)
    return sizes[jax.random.permutation(jax.random.fold_in(rng, 2), number_of)]


def centred(rng, extent, width, most, pieces=(), dtype=jnp.bfloat16):
    values = jax.random.normal(rng, extent, jnp.float32) * width
    if len(pieces) > 0:
        values = block_levels(rng, extent, pieces, -0.22, 0.18) * values
    return jnp.clip(values, min=-most, max=most).astype(dtype)


def setup_inputs(seed: int = 0) -> dict:
    key_of = jax.random.split(jax.random.key(seed), 8)
    hidden = centred(key_of[0], (TOKEN_TOTAL, D), 1.0, 6.0, ((0, 768),))
    doc_ids = jax.vmap(lambda own: jnp.searchsorted(jnp.cumsum(uneven_parts(own, DOCS, TOK_DEV, MOST_DOC, 2)), jnp.arange(TOK_DEV), side="right"))(jax.random.split(key_of[1], N_DP)).reshape((N_DP, TOK_DEV)).astype(jnp.int32)
    teacher = centred(key_of[2], (TOKEN_TOTAL, P_SIZE), 1.0, 6.0, ((0, 128), (1, 6)))
    rotation = jax.random.randint(key_of[3], (1,), 0, N_DP).astype(jnp.int32)
    norm_gain_vector = jnp.clip(1.0 + 0.1 * jax.random.normal(key_of[4], (D,), jnp.float32), 0.5, 1.5)
    proj_bias = centred(key_of[5], (P_SIZE,), 0.5, 3.0, ((0, 6),), jnp.float32)
    projection = centred(key_of[6], (D, P_SIZE), D ** -0.5, 0.09375, ((1, 6),))
    return dict(hidden=hidden, doc_ids=doc_ids, teacher=teacher, rotation=rotation, norm_gain_vector=norm_gain_vector, proj_bias=proj_bias, projection=projection)


norm_eps = 1e-05

def reference(hidden, doc_ids, teacher, rotation, norm_gain_vector, proj_bias, projection):
    value_entries = hidden.astype(jnp.float32)
    mean_sq = lax.optimization_barrier(jnp.mean(value_entries * value_entries, axis=-1, keepdims=True))
    inverse_root_mean = lax.rsqrt(mean_sq + norm_eps)
    unscaled_rows = value_entries * inverse_root_mean
    normalized_rows = (unscaled_rows * norm_gain_vector).astype(jnp.bfloat16)
    logits = jnp.dot(normalized_rows, projection, preferred_element_type=jnp.float32) + proj_bias
    shift_rows = (rotation[0] * TOK_DEV).astype(jnp.int32)
    target = jnp.roll(teacher, -shift_rows, axis=0).astype(jnp.float32)
    same_doc = lax.optimization_barrier(jnp.sum((doc_ids[:, :, None] == doc_ids[:, None, :]).astype(jnp.float32), axis=-1))
    weight = (TOK_DEV / (DOCS * same_doc)).reshape(-1)[:, None]
    error_rows = logits - target
    distill_loss = jnp.sum(weight * error_rows * error_rows) / (2.0 * TOKEN_TOTAL * P_SIZE)
    grad_out = (weight * error_rows).astype(jnp.bfloat16)
    grad_bias = lax.optimization_barrier(jnp.sum(grad_out.astype(jnp.float32), axis=0)) / TOKEN_TOTAL
    normalized_gradient = lax.dot_general(grad_out, projection, (((1,), (1,)), ((), ())), preferred_element_type=jnp.float32)
    gain_gradient_mean = lax.optimization_barrier(jnp.sum(normalized_gradient * unscaled_rows, axis=0)) / TOKEN_TOTAL
    unscaled_gradient = normalized_gradient * norm_gain_vector
    inner_product = lax.optimization_barrier(jnp.mean(unscaled_gradient * unscaled_rows, axis=-1, keepdims=True))
    hidden_gradient = (inverse_root_mean * (unscaled_gradient - unscaled_rows * inner_product)).astype(jnp.bfloat16)
    return (hidden_gradient, gain_gradient_mean, grad_bias, distill_loss)
```

```python
import jax
import jax.numpy as jnp
import numpy as np
from jax import lax
from jax.sharding import Mesh, PartitionSpec as P

DOCS = 4
NORM_EPS = 1e-05

AXES = ("x", "y", "zh", "zl", "c")
SIZES = (4, 8, 4, 3, 2)
DP = ("x", "y", "zh")
TENSOR = ("zl", "c")
N_X, N_Y, N_ZH, N_ZL, N_C = SIZES
N_DP = N_X * N_Y * N_ZH
LANES = 128


def pull(value, steps):
    return lax.ppermute(value, DP, [((i + steps) % N_DP, i) for i in range(N_DP)])


def swap_cores(value):
    return lax.ppermute(value, "c", [(0, 1), (1, 0)])


def spread(value, axes, count):
    copies = lax.optimization_barrier(jnp.broadcast_to(value[None], (count, *value.shape)))
    return lax.all_to_all(copies, axes, 0, 0, tiled=True)


def own_first(value, core):
    parts = value.reshape(N_ZL, N_C, -1, *value.shape[1:])
    half = (value.shape[0] // N_C, *value.shape[1:])
    even, odd = parts[:, 0].reshape(half), parts[:, 1].reshape(half)
    first = core == 0
    return jnp.concatenate([jnp.where(first, even, odd), jnp.where(first, odd, even)], 0)


def normalized(rows):
    entries = rows.astype(jnp.float32)
    inverse = lax.rsqrt(jnp.mean(entries * entries, axis=-1, keepdims=True) + NORM_EPS)
    return entries * inverse, inverse


def shards(hidden, doc_ids, teacher, rotation, gain, bias, projection):
    core = lax.axis_index("c")
    here = (lax.axis_index("x") * N_Y + lax.axis_index("y")) * N_ZH + lax.axis_index("zh")
    turn = rotation[0] % N_DP
    portion_rows, width = hidden.shape
    block_rows = teacher.shape[0]
    columns = projection.shape[1]
    tokens = block_rows * N_DP
    features = columns * N_ZL * N_C

    gathered = spread(hidden, "zl", N_ZL)

    far = [lambda t, s=s: pull(t, s * N_ZH) if s else t for s in range(N_X * N_Y)]
    moved = lax.switch(turn // N_ZH, far, teacher)

    def near(step):
        def branch(t, mine):
            target = pull(t, step) if step else t
            mine = mine.reshape(-1, width)
            block = jnp.concatenate([mine, swap_cores(mine)], 0)
            unscaled, _ = normalized(block)
            rows = (unscaled * gain).astype(jnp.bfloat16)
            logits = jnp.dot(rows, projection, preferred_element_type=jnp.float32) + bias
            return target, logits, block

        return branch

    target, logits, block = lax.switch(turn % N_ZH, [near(s) for s in range(N_ZH)], moved, gathered)

    row_docs = lax.dynamic_slice_in_dim(doc_ids, here, 1, 0)[0]
    same_doc = jnp.sum((row_docs[:, None] == row_docs[None, :]).astype(jnp.float32), axis=-1)
    weight = own_first((block_rows / (DOCS * same_doc))[:, None], core)
    error = logits - own_first(target, core).astype(jnp.float32)
    loss_part = jnp.sum(weight * error * error) / (2.0 * tokens * features)
    grad_out = (weight * error).astype(jnp.bfloat16)
    bias_part = jnp.sum(grad_out.astype(jnp.float32), axis=0) / tokens
    grad_all = lax.dot_general(
        grad_out, projection, (((1,), (1,)), ((), ())), preferred_element_type=jnp.float32
    )
    block_unscaled, _ = normalized(block)
    gain_part = jnp.sum(grad_all * block_unscaled, axis=0) / tokens

    half = block_rows // N_C
    summed = grad_all[:half] + swap_cores(grad_all[half:].astype(jnp.bfloat16)).astype(jnp.float32)
    pieces = summed.astype(jnp.bfloat16).reshape(N_ZL, portion_rows, width)
    pieces = lax.all_to_all(pieces, "zl", 0, 0, tiled=True)
    portion_gradient = jnp.sum(pieces.astype(jnp.float32), axis=0)

    gain_lines, bias_lines = width // LANES, columns // LANES
    total_lines = -(-(gain_lines + 1 + bias_lines) // 8) * 8
    vector = jnp.concatenate(
        [
            gain_part.reshape(gain_lines, LANES),
            jnp.broadcast_to(loss_part, (1, LANES)),
            bias_part.reshape(bias_lines, LANES),
            jnp.zeros((total_lines - gain_lines - 1 - bias_lines, LANES), jnp.float32),
        ],
        0,
    )
    over_tensor = jnp.sum(spread(vector, TENSOR, N_ZL * N_C), axis=0)
    shared = lax.broadcasted_iota(jnp.int32, vector.shape, 0) < gain_lines + 1
    vector = jnp.where(shared, over_tensor, vector)
    for axis, count in (("x", N_X), ("y", N_Y), ("zh", N_ZH)):
        vector = jnp.sum(spread(vector, axis, count), axis=0)
    gain_gradient_mean = vector[:gain_lines].reshape(width)
    distill_loss = vector[gain_lines, 0]
    grad_bias = vector[gain_lines + 1 : gain_lines + 1 + bias_lines].reshape(columns)

    unscaled, inverse = normalized(hidden)
    unscaled_gradient = portion_gradient * gain
    inner = jnp.mean(unscaled_gradient * unscaled, axis=-1, keepdims=True)
    hidden_gradient = (inverse * (unscaled_gradient - unscaled * inner)).astype(jnp.bfloat16)
    return (hidden_gradient, gain_gradient_mean, grad_bias, distill_loss)


def solution(mesh):
    split = Mesh(np.asarray(mesh.devices).reshape(SIZES), AXES)
    return jax.shard_map(
        shards,
        mesh=split,
        in_specs=(P(AXES, None), P(), P(DP, TENSOR), P(), P(), P(TENSOR), P(None, TENSOR)),
        out_specs=(P(AXES, None), P(), P(TENSOR), P()),
        check_vma=False,
    )
```

```python
import jax
import jax.numpy as jnp
import numpy as np
from jax import lax
from jax.sharding import Mesh, PartitionSpec as P


DOCS = 4
NORM_EPS = 1e-05

AXES = ("x", "y", "zh", "zl", "c")
SIZES = (4, 8, 4, 3, 2)
DP = ("x", "y", "zh")
TENSOR = ("zl", "c")
N_X, N_Y, N_ZH, N_ZL, N_C = SIZES
N_DP = N_X * N_Y * N_ZH
LANES = 128


def pull(value, steps):
    return lax.ppermute(value, DP, [((i + steps) % N_DP, i) for i in range(N_DP)])


def swap_cores(value):
    return lax.ppermute(value, "c", [(0, 1), (1, 0)])


def spread(value, axes, count):
    copies = lax.optimization_barrier(jnp.broadcast_to(value[None], (count, *value.shape)))
    return lax.all_to_all(copies, axes, 0, 0, tiled=True)


def own_first(value, core):
    parts = value.reshape(N_ZL, N_C, -1, *value.shape[1:])
    half = (value.shape[0] // N_C, *value.shape[1:])
    even, odd = parts[:, 0].reshape(half), parts[:, 1].reshape(half)
    first = core == 0
    return jnp.concatenate([jnp.where(first, even, odd), jnp.where(first, odd, even)], 0)


def normalized(rows):
    entries = rows.astype(jnp.float32)
    inverse = lax.rsqrt(jnp.mean(entries * entries, axis=-1, keepdims=True) + NORM_EPS)
    return entries * inverse, inverse


def shards(hidden, doc_ids, teacher, rotation, gain, bias, projection):
    core = lax.axis_index("c")
    here = (lax.axis_index("x") * N_Y + lax.axis_index("y")) * N_ZH + lax.axis_index("zh")
    turn = rotation[0] % N_DP
    portion_rows, width = hidden.shape
    block_rows = teacher.shape[0]
    columns = projection.shape[1]
    tokens = block_rows * N_DP
    features = columns * N_ZL * N_C

    gathered = spread(hidden, "zl", N_ZL)

    far = [lambda t, s=s: pull(t, s * N_ZH) if s else t for s in range(N_X * N_Y)]
    moved = lax.switch(turn // N_ZH, far, teacher)

    row_docs = lax.dynamic_slice_in_dim(doc_ids, here, 1, 0)[0]
    same_doc = jnp.sum((row_docs[:, None] == row_docs[None, :]).astype(jnp.float32), axis=-1)
    weight = own_first((block_rows / (DOCS * same_doc))[:, None], core)

    def near(step):
        def branch(t, mine, weight):
            target = pull(t, step) if step else t
            mine = mine.reshape(-1, width)
            other = swap_cores(mine)
            block = jnp.concatenate([mine, other], 0)
            unscaled, inverse = normalized(block)
            rows = (unscaled * gain).astype(jnp.bfloat16)
            logits = jnp.dot(rows, projection, preferred_element_type=jnp.float32) + bias
            logits = lax.optimization_barrier(logits)
            error = logits - own_first(target, core).astype(jnp.float32)
            loss_part = jnp.sum(weight * error * error) / (2.0 * tokens * features)
            grad_out = (weight * error).astype(jnp.bfloat16)
            bias_part = jnp.sum(grad_out.astype(jnp.float32), axis=0) / tokens
            return lax.optimization_barrier((grad_out, loss_part, bias_part, other, inverse))

        return branch

    grad_out, loss_part, bias_part, other, block_inverse = lax.switch(
        turn % N_ZH, [near(s) for s in range(N_ZH)], moved, gathered, weight
    )
    grad_all = lax.dot_general(
        grad_out, projection, (((1,), (1,)), ((), ())), preferred_element_type=jnp.float32
    )
    block = jnp.concatenate([gathered.reshape(-1, width), other], 0)
    gain_part = jnp.sum(grad_all * (block.astype(jnp.float32) * block_inverse), axis=0) / tokens

    half = block_rows // N_C
    summed = grad_all[:half] + swap_cores(grad_all[half:].astype(jnp.bfloat16)).astype(jnp.float32)
    summed = summed.reshape(N_ZL, portion_rows, width)
    at = lax.axis_index("zl")
    portion_gradient = lax.dynamic_index_in_dim(summed, at, 0, keepdims=False)
    for step in range(1, N_ZL):
        piece = lax.dynamic_index_in_dim(summed, (at + step) % N_ZL, 0, keepdims=False)
        ring = [(i, (i + step) % N_ZL) for i in range(N_ZL)]
        piece = lax.ppermute(piece.astype(jnp.bfloat16), "zl", ring)
        portion_gradient = portion_gradient + piece.astype(jnp.float32)

    n_tensor = N_ZL * N_C
    peers = N_X * n_tensor
    gain_lines, bias_lines = width // LANES, columns // LANES
    gain_each, bias_each = -(-(gain_lines + 1) // peers), -(-bias_lines // N_X)
    used = gain_each + bias_each
    each = -(-used // 8) * 8
    shared = jnp.concatenate(
        [
            gain_part.reshape(gain_lines, LANES),
            jnp.broadcast_to(loss_part, (1, LANES)),
            jnp.zeros((peers * gain_each - gain_lines - 1, LANES), jnp.float32),
        ],
        0,
    ).reshape(peers, gain_each, LANES)
    by_x = jnp.pad(bias_part.reshape(bias_lines, LANES), ((0, N_X * bias_each - bias_lines), (0, 0)))
    by_x = jnp.broadcast_to(by_x.reshape(N_X, 1, bias_each, LANES), (N_X, n_tensor, bias_each, LANES))
    lines = jnp.concatenate(
        [
            shared,
            by_x.reshape(peers, bias_each, LANES),
            jnp.zeros((peers, each - used, LANES), jnp.float32),
        ],
        1,
    )
    group = ("x", *TENSOR)
    column = lax.axis_index("zl") * N_C + core
    lines = lax.all_to_all(lines, group, 0, 0, tiled=True)
    line = lax.broadcasted_iota(jnp.int32, lines.shape, 1)
    sender = lax.broadcasted_iota(jnp.int32, lines.shape, 0) % n_tensor
    lines = jnp.sum(jnp.where((line < gain_each) | (sender == column), lines, 0.0), axis=0)
    lines = jnp.sum(spread(lines, ("y", "zh"), N_Y * N_ZH), axis=0)
    lines = spread(lines, group, peers)
    shared = lines[:, :gain_each].reshape(peers * gain_each, LANES)
    gain_gradient_mean = shared[:gain_lines].reshape(width)
    distill_loss = shared[gain_lines, 0]
    by_x = lax.dynamic_slice_in_dim(
        lines[:, gain_each:used].reshape(N_X, n_tensor, bias_each, LANES), column, 1, 1
    )
    grad_bias = by_x.reshape(N_X * bias_each, LANES)[:bias_lines].reshape(columns)

    unscaled, inverse = normalized(hidden)
    unscaled_gradient = portion_gradient * gain
    inner = jnp.mean(unscaled_gradient * unscaled, axis=-1, keepdims=True)
    hidden_gradient = (inverse * (unscaled_gradient - unscaled * inner)).astype(jnp.bfloat16)
    return (hidden_gradient, gain_gradient_mean, grad_bias, distill_loss)


def solution(mesh):
    split = Mesh(np.asarray(mesh.devices).reshape(SIZES), AXES)
    return jax.shard_map(
        shards,
        mesh=split,
        in_specs=(P(AXES, None), P(), P(DP, TENSOR), P(), P(), P(TENSOR), P(None, TENSOR)),
        out_specs=(P(AXES, None), P(), P(TENSOR), P()),
        check_vma=False,
    )
```

```python
import jax
import jax.numpy as jnp
import numpy as np
from jax import lax
from jax.experimental import pallas as pl
from jax.sharding import Mesh, PartitionSpec as P


DOCS = 4
NORM_EPS = 1e-05

AXES = ("x", "y", "zh", "zl", "c")
SIZES = (4, 8, 4, 3, 2)
DP = ("x", "y", "zh")
TENSOR = ("zl", "c")
N_X, N_Y, N_ZH, N_ZL, N_C = SIZES
N_DP = N_X * N_Y * N_ZH
LANES = 128
BLOCK = 512
INTERPRET = False


def pull(value, steps):
    return lax.ppermute(value, DP, [((i + steps) % N_DP, i) for i in range(N_DP)])


def swap_cores(value):
    return lax.ppermute(value, "c", [(0, 1), (1, 0)])


def spread(value, axes, count):
    copies = lax.optimization_barrier(jnp.broadcast_to(value[None], (count, *value.shape)))
    return lax.all_to_all(copies, axes, 0, 0, tiled=True)


def own_first(value, core):
    parts = value.reshape(N_ZL, N_C, -1, *value.shape[1:])
    half = (value.shape[0] // N_C, *value.shape[1:])
    even, odd = parts[:, 0].reshape(half), parts[:, 1].reshape(half)
    first = core == 0
    return jnp.concatenate([jnp.where(first, even, odd), jnp.where(first, odd, even)], 0)


def normalized(rows):
    entries = rows.astype(jnp.float32)
    inverse = lax.rsqrt(jnp.mean(entries * entries, axis=-1, keepdims=True) + NORM_EPS)
    return entries * inverse, inverse


def back_body(grad_ref, weights_ref, mine_ref, other_ref, inverse_ref, own_ref, far_ref, gain_ref):
    half = mine_ref.shape[0]
    grads = lax.dot_general(
        grad_ref[...], weights_ref[...], (((1,), (1,)), ((), ())), preferred_element_type=jnp.float32
    )
    own, far = grads[:half], grads[half:]
    own_ref[...] = own
    far_ref[...] = far.astype(jnp.bfloat16)
    here = own * (mine_ref[...].astype(jnp.float32) * inverse_ref[:half])
    there = far * (other_ref[...].astype(jnp.float32) * inverse_ref[half:])
    gain_ref[...] = jnp.sum(here + there, axis=0, keepdims=True)


def back(grad_out, weights, mine, other, inverse):
    rows, columns = grad_out.shape
    half, width = mine.shape
    block = BLOCK
    while width % block:
        block //= 2
    whole = lambda i: (0, 0)
    along = lambda i: (0, i)
    return pl.pallas_call(
        back_body,
        grid=(width // block,),
        in_specs=[
            pl.BlockSpec((rows, columns), whole),
            pl.BlockSpec((block, columns), lambda i: (i, 0)),
            pl.BlockSpec((half, block), along),
            pl.BlockSpec((half, block), along),
            pl.BlockSpec((rows, 1), whole),
        ],
        out_specs=[
            pl.BlockSpec((half, block), along),
            pl.BlockSpec((half, block), along),
            pl.BlockSpec((1, block), along),
        ],
        out_shape=[
            jax.ShapeDtypeStruct((half, width), jnp.float32),
            jax.ShapeDtypeStruct((half, width), jnp.bfloat16),
            jax.ShapeDtypeStruct((1, width), jnp.float32),
        ],
        cost_estimate=pl.CostEstimate(
            flops=2 * rows * columns * width,
            bytes_accessed=2 * columns * width + 10 * half * width,
            transcendentals=0,
        ),
        name="back",
        interpret=INTERPRET,
    )(grad_out, weights, mine, other, inverse)


def shards(hidden, doc_ids, teacher, rotation, gain, bias, projection):
    core = lax.axis_index("c")
    here = (lax.axis_index("x") * N_Y + lax.axis_index("y")) * N_ZH + lax.axis_index("zh")
    turn = rotation[0] % N_DP
    portion_rows, width = hidden.shape
    block_rows = teacher.shape[0]
    columns = projection.shape[1]
    tokens = block_rows * N_DP
    features = columns * N_ZL * N_C

    gathered = spread(hidden, "zl", N_ZL)

    far = [lambda t, s=s: pull(t, s * N_ZH) if s else t for s in range(N_X * N_Y)]
    moved = lax.switch(turn // N_ZH, far, teacher)

    row_docs = lax.dynamic_slice_in_dim(doc_ids, here, 1, 0)[0]
    same_doc = jnp.sum((row_docs[:, None] == row_docs[None, :]).astype(jnp.float32), axis=-1)
    weight = own_first((block_rows / (DOCS * same_doc))[:, None], core)

    def near(step):
        def branch(t, mine, weight):
            target = pull(t, step) if step else t
            mine = mine.reshape(-1, width)
            other = swap_cores(mine)
            block = jnp.concatenate([mine, other], 0)
            unscaled, inverse = normalized(block)
            rows = (unscaled * gain).astype(jnp.bfloat16)
            logits = jnp.dot(rows, projection, preferred_element_type=jnp.float32) + bias
            logits = lax.optimization_barrier(logits)
            error = logits - own_first(target, core).astype(jnp.float32)
            loss_part = jnp.sum(weight * error * error) / (2.0 * tokens * features)
            grad_out = (weight * error).astype(jnp.bfloat16)
            bias_part = jnp.sum(grad_out.astype(jnp.float32), axis=0) / tokens
            return lax.optimization_barrier((grad_out, loss_part, bias_part, other, inverse))

        return branch

    grad_out, loss_part, bias_part, other, block_inverse = lax.switch(
        turn % N_ZH, [near(s) for s in range(N_ZH)], moved, gathered, weight
    )
    own_rows, far_rows, gain_part = back(
        grad_out, projection, gathered.reshape(-1, width), other, block_inverse
    )
    gain_part = gain_part / tokens
    summed = own_rows + swap_cores(far_rows).astype(jnp.float32)
    summed = summed.reshape(N_ZL, portion_rows, width)
    at = lax.axis_index("zl")
    portion_gradient = lax.dynamic_index_in_dim(summed, at, 0, keepdims=False)
    pieces = []
    for step in range(1, N_ZL):
        piece = lax.dynamic_index_in_dim(summed, (at + step) % N_ZL, 0, keepdims=False)
        ring = [(i, (i + step) % N_ZL) for i in range(N_ZL)]
        pieces.append(lax.ppermute(piece.astype(jnp.bfloat16), "zl", ring))

    n_tensor = N_ZL * N_C
    peers = N_X * n_tensor
    gain_lines, bias_lines = width // LANES, columns // LANES
    gain_each, bias_each = -(-(gain_lines + 1) // peers), -(-bias_lines // N_X)
    used = gain_each + bias_each
    each = -(-used // 8) * 8
    shared = jnp.concatenate(
        [
            gain_part.reshape(gain_lines, LANES),
            jnp.broadcast_to(loss_part, (1, LANES)),
            jnp.zeros((peers * gain_each - gain_lines - 1, LANES), jnp.float32),
        ],
        0,
    ).reshape(peers, gain_each, LANES)
    by_x = jnp.pad(bias_part.reshape(bias_lines, LANES), ((0, N_X * bias_each - bias_lines), (0, 0)))
    by_x = jnp.broadcast_to(by_x.reshape(N_X, 1, bias_each, LANES), (N_X, n_tensor, bias_each, LANES))
    lines = jnp.concatenate(
        [
            shared,
            by_x.reshape(peers, bias_each, LANES),
            jnp.zeros((peers, each - used, LANES), jnp.float32),
        ],
        1,
    )
    group = ("x", *TENSOR)
    column = lax.axis_index("zl") * N_C + core
    lines = lax.all_to_all(lines, group, 0, 0, tiled=True)
    line = lax.broadcasted_iota(jnp.int32, lines.shape, 1)
    sender = lax.broadcasted_iota(jnp.int32, lines.shape, 0) % n_tensor
    lines = jnp.sum(jnp.where((line < gain_each) | (sender == column), lines, 0.0), axis=0)
    lines = jnp.sum(spread(lines, ("y", "zh"), N_Y * N_ZH), axis=0)
    lines = spread(lines, group, peers)
    shared = lines[:, :gain_each].reshape(peers * gain_each, LANES)
    gain_gradient_mean = shared[:gain_lines].reshape(width)
    distill_loss = shared[gain_lines, 0]
    by_x = lax.dynamic_slice_in_dim(
        lines[:, gain_each:used].reshape(N_X, n_tensor, bias_each, LANES), column, 1, 1
    )
    grad_bias = by_x.reshape(N_X * bias_each, LANES)[:bias_lines].reshape(columns)

    unscaled, inverse = normalized(hidden)
    for piece in pieces:
        portion_gradient = portion_gradient + piece.astype(jnp.float32)
    unscaled_gradient = portion_gradient * gain
    inner = jnp.mean(unscaled_gradient * unscaled, axis=-1, keepdims=True)
    hidden_gradient = (inverse * (unscaled_gradient - unscaled * inner)).astype(jnp.bfloat16)
    return (hidden_gradient, gain_gradient_mean, grad_bias, distill_loss)


def solution(mesh):
    split = Mesh(np.asarray(mesh.devices).reshape(SIZES), AXES)
    return jax.shard_map(
        shards,
        mesh=split,
        in_specs=(P(AXES, None), P(), P(DP, TENSOR), P(), P(), P(TENSOR), P(None, TENSOR)),
        out_specs=(P(AXES, None), P(), P(TENSOR), P()),
        check_vma=False,
    )
```

```python
import jax
import jax.numpy as jnp
import numpy as np
from jax import lax
from jax.sharding import Mesh, PartitionSpec as P


DOCS = 4
NORM_EPS = 1e-05

AXES = ("x", "y", "zh", "zl", "c")
SIZES = (4, 8, 4, 3, 2)
DP = ("x", "y", "zh")
TENSOR = ("zl", "c")
N_X, N_Y, N_ZH, N_ZL, N_C = SIZES
N_DP = N_X * N_Y * N_ZH
LANES = 128


def pull(value, steps):
    return lax.ppermute(value, DP, [((i + steps) % N_DP, i) for i in range(N_DP)])


def swap_cores(value):
    return lax.ppermute(value, "c", [(0, 1), (1, 0)])


def spread(value, axes, count):
    copies = lax.optimization_barrier(jnp.broadcast_to(value[None], (count, *value.shape)))
    return lax.all_to_all(copies, axes, 0, 0, tiled=True)


def own_first(value, core):
    parts = value.reshape(N_ZL, N_C, -1, *value.shape[1:])
    half = (value.shape[0] // N_C, *value.shape[1:])
    even, odd = parts[:, 0].reshape(half), parts[:, 1].reshape(half)
    first = core == 0
    return jnp.concatenate([jnp.where(first, even, odd), jnp.where(first, odd, even)], 0)


def normalized(rows):
    entries = rows.astype(jnp.float32)
    inverse = lax.rsqrt(jnp.mean(entries * entries, axis=-1, keepdims=True) + NORM_EPS)
    return entries * inverse, inverse


def shards(hidden, doc_ids, teacher, rotation, gain, bias, projection):
    core = lax.axis_index("c")
    here = (lax.axis_index("x") * N_Y + lax.axis_index("y")) * N_ZH + lax.axis_index("zh")
    turn = rotation[0] % N_DP
    portion_rows, width = hidden.shape
    block_rows = teacher.shape[0]
    columns = projection.shape[1]
    tokens = block_rows * N_DP
    features = columns * N_ZL * N_C

    gathered = spread(hidden, "zl", N_ZL)

    far = [lambda t, s=s: pull(t, s * N_ZH) if s else t for s in range(N_X * N_Y)]
    moved = lax.switch(turn // N_ZH, far, teacher)

    row_docs = lax.dynamic_slice_in_dim(doc_ids, here, 1, 0)[0]
    same_doc = jnp.sum((row_docs[:, None] == row_docs[None, :]).astype(jnp.float32), axis=-1)
    weight = own_first((block_rows / (DOCS * same_doc))[:, None], core)

    def near(step):
        def branch(t, mine, weight):
            target = pull(t, step) if step else t
            mine = mine.reshape(-1, width)
            other = swap_cores(mine)
            block = jnp.concatenate([mine, other], 0)
            unscaled, inverse = normalized(block)
            rows = (unscaled * gain).astype(jnp.bfloat16)
            logits = jnp.dot(rows, projection, preferred_element_type=jnp.float32) + bias
            logits = lax.optimization_barrier(logits)
            error = logits - own_first(target, core).astype(jnp.float32)
            loss_part = jnp.sum(weight * error * error) / (2.0 * tokens * features)
            grad_out = (weight * error).astype(jnp.bfloat16)
            bias_part = jnp.sum(grad_out.astype(jnp.float32), axis=0) / tokens
            return lax.optimization_barrier((grad_out, loss_part, bias_part, other, inverse))

        return branch

    grad_out, loss_part, bias_part, other, block_inverse = lax.switch(
        turn % N_ZH, [near(s) for s in range(N_ZH)], moved, gathered, weight
    )
    grad_all = lax.dot_general(
        grad_out, projection, (((1,), (1,)), ((), ())), preferred_element_type=jnp.float32
    )
    grad_all = lax.optimization_barrier(grad_all)
    block = jnp.concatenate([gathered.reshape(-1, width), other], 0)
    gain_part = jnp.sum(grad_all * (block.astype(jnp.float32) * block_inverse), axis=0) / tokens
    half = block_rows // N_C
    own_rows, far_rows = grad_all[:half], grad_all[half:].astype(jnp.bfloat16)
    summed = own_rows + swap_cores(far_rows).astype(jnp.float32)
    summed = summed.reshape(N_ZL, portion_rows, width)
    at = lax.axis_index("zl")
    portion_gradient = lax.dynamic_index_in_dim(summed, at, 0, keepdims=False)
    pieces = []
    for step in range(1, N_ZL):
        piece = lax.dynamic_index_in_dim(summed, (at + step) % N_ZL, 0, keepdims=False)
        ring = [(i, (i + step) % N_ZL) for i in range(N_ZL)]
        pieces.append(lax.ppermute(piece.astype(jnp.bfloat16), "zl", ring))

    n_tensor = N_ZL * N_C
    peers = N_X * n_tensor
    gain_lines, bias_lines = width // LANES, columns // LANES
    gain_each, bias_each = -(-(gain_lines + 1) // peers), -(-bias_lines // N_X)
    used = gain_each + bias_each
    each = -(-used // 8) * 8
    shared = jnp.concatenate(
        [
            gain_part.reshape(gain_lines, LANES),
            jnp.broadcast_to(loss_part, (1, LANES)),
            jnp.zeros((peers * gain_each - gain_lines - 1, LANES), jnp.float32),
        ],
        0,
    ).reshape(peers, gain_each, LANES)
    by_x = jnp.pad(bias_part.reshape(bias_lines, LANES), ((0, N_X * bias_each - bias_lines), (0, 0)))
    by_x = jnp.broadcast_to(by_x.reshape(N_X, 1, bias_each, LANES), (N_X, n_tensor, bias_each, LANES))
    lines = jnp.concatenate(
        [
            shared,
            by_x.reshape(peers, bias_each, LANES),
            jnp.zeros((peers, each - used, LANES), jnp.float32),
        ],
        1,
    )
    group = ("x", *TENSOR)
    column = lax.axis_index("zl") * N_C + core
    lines = lax.all_to_all(lines, group, 0, 0, tiled=True)
    line = lax.broadcasted_iota(jnp.int32, lines.shape, 1)
    sender = lax.broadcasted_iota(jnp.int32, lines.shape, 0) % n_tensor
    lines = jnp.sum(jnp.where((line < gain_each) | (sender == column), lines, 0.0), axis=0)
    lines = jnp.sum(spread(lines, ("y", "zh"), N_Y * N_ZH), axis=0)
    lines = spread(lines, group, peers)
    shared = lines[:, :gain_each].reshape(peers * gain_each, LANES)
    gain_gradient_mean = shared[:gain_lines].reshape(width)
    distill_loss = shared[gain_lines, 0]
    by_x = lax.dynamic_slice_in_dim(
        lines[:, gain_each:used].reshape(N_X, n_tensor, bias_each, LANES), column, 1, 1
    )
    grad_bias = by_x.reshape(N_X * bias_each, LANES)[:bias_lines].reshape(columns)

    unscaled, inverse = normalized(hidden)
    for piece in pieces:
        portion_gradient = portion_gradient + piece.astype(jnp.float32)
    unscaled_gradient = portion_gradient * gain
    inner = jnp.mean(unscaled_gradient * unscaled, axis=-1, keepdims=True)
    hidden_gradient = (inverse * (unscaled_gradient - unscaled * inner)).astype(jnp.bfloat16)
    return (hidden_gradient, gain_gradient_mean, grad_bias, distill_loss)


def solution(mesh):
    split = Mesh(np.asarray(mesh.devices).reshape(SIZES), AXES)
    return jax.shard_map(
        shards,
        mesh=split,
        in_specs=(P(AXES, None), P(), P(DP, TENSOR), P(), P(), P(TENSOR), P(None, TENSOR)),
        out_specs=(P(AXES, None), P(), P(TENSOR), P()),
        check_vma=False,
    )
```

```python
import jax
import jax.numpy as jnp
import numpy as np
from jax import lax
from jax.sharding import Mesh, PartitionSpec as P


DOCS = 4
NORM_EPS = 1e-05

AXES = ("x", "y", "zh", "zl", "c")
SIZES = (4, 8, 4, 3, 2)
DP = ("x", "y", "zh")
TENSOR = ("zl", "c")
N_X, N_Y, N_ZH, N_ZL, N_C = SIZES
N_DP = N_X * N_Y * N_ZH
LANES = 128


def pull(value, steps):
    return lax.ppermute(value, DP, [((i + steps) % N_DP, i) for i in range(N_DP)])


def swap_cores(value):
    return lax.ppermute(value, "c", [(0, 1), (1, 0)])


def spread(value, axes, count):
    copies = lax.optimization_barrier(jnp.broadcast_to(value[None], (count, *value.shape)))
    return lax.all_to_all(copies, axes, 0, 0, tiled=True)


def own_first(value, core):
    parts = value.reshape(N_ZL, N_C, -1, *value.shape[1:])
    half = (value.shape[0] // N_C, *value.shape[1:])
    even, odd = parts[:, 0].reshape(half), parts[:, 1].reshape(half)
    first = core == 0
    return jnp.concatenate([jnp.where(first, even, odd), jnp.where(first, odd, even)], 0)


def normalized(rows):
    entries = rows.astype(jnp.float32)
    inverse = lax.rsqrt(jnp.mean(entries * entries, axis=-1, keepdims=True) + NORM_EPS)
    return entries * inverse, inverse


def shards(hidden, doc_ids, teacher, rotation, gain, bias, projection):
    core = lax.axis_index("c")
    here = (lax.axis_index("x") * N_Y + lax.axis_index("y")) * N_ZH + lax.axis_index("zh")
    turn = rotation[0] % N_DP
    portion_rows, width = hidden.shape
    block_rows = teacher.shape[0]
    columns = projection.shape[1]
    tokens = block_rows * N_DP
    features = columns * N_ZL * N_C

    gathered = spread(hidden, "zl", N_ZL)

    far = [lambda t, s=s: pull(t, s * N_ZH) if s else t for s in range(N_X * N_Y)]
    moved = lax.switch(turn // N_ZH, far, teacher)

    row_docs = lax.dynamic_slice_in_dim(doc_ids, here, 1, 0)[0]
    same_doc = jnp.sum((row_docs[:, None] == row_docs[None, :]).astype(jnp.float32), axis=-1)
    weight = own_first((block_rows / (DOCS * same_doc))[:, None], core)

    def near(step):
        def branch(t, mine, weight):
            target = pull(t, step) if step else t
            mine = mine.reshape(-1, width)
            other = swap_cores(mine)
            block = jnp.concatenate([mine, other], 0)
            unscaled, inverse = normalized(block)
            rows = (unscaled * gain).astype(jnp.bfloat16)
            logits = jnp.dot(rows, projection, preferred_element_type=jnp.float32) + bias
            logits = lax.optimization_barrier(logits)
            error = logits - own_first(target, core).astype(jnp.float32)
            loss_part = jnp.sum(weight * error * error) / (2.0 * tokens * features)
            grad_out = (weight * error).astype(jnp.bfloat16)
            bias_part = jnp.sum(grad_out.astype(jnp.float32), axis=0) / tokens
            grad_all = lax.dot_general(
                grad_out, projection, (((1,), (1,)), ((), ())), preferred_element_type=jnp.float32
            )
            return lax.optimization_barrier((grad_all, loss_part, bias_part, other, inverse))

        return branch

    grad_all, loss_part, bias_part, other, block_inverse = lax.switch(
        turn % N_ZH, [near(s) for s in range(N_ZH)], moved, gathered, weight
    )
    block = jnp.concatenate([gathered.reshape(-1, width), other], 0)
    gain_part = jnp.sum(grad_all * (block.astype(jnp.float32) * block_inverse), axis=0) / tokens
    half = block_rows // N_C
    own_rows = grad_all[:half]
    far_rows = grad_all[half:].astype(jnp.bfloat16)
    summed = own_rows + swap_cores(far_rows).astype(jnp.float32)
    summed = summed.reshape(N_ZL, portion_rows, width)
    at = lax.axis_index("zl")
    portion_gradient = lax.dynamic_index_in_dim(summed, at, 0, keepdims=False)
    pieces = []
    for step in range(1, N_ZL):
        piece = lax.dynamic_index_in_dim(summed, (at + step) % N_ZL, 0, keepdims=False)
        ring = [(i, (i + step) % N_ZL) for i in range(N_ZL)]
        pieces.append(lax.ppermute(piece.astype(jnp.bfloat16), "zl", ring))

    n_tensor = N_ZL * N_C
    peers = N_X * n_tensor
    gain_lines, bias_lines = width // LANES, columns // LANES
    gain_each, bias_each = -(-(gain_lines + 1) // peers), -(-bias_lines // N_X)
    used = gain_each + bias_each
    each = -(-used // 8) * 8
    shared = jnp.concatenate(
        [
            gain_part.reshape(gain_lines, LANES),
            jnp.broadcast_to(loss_part, (1, LANES)),
            jnp.zeros((peers * gain_each - gain_lines - 1, LANES), jnp.float32),
        ],
        0,
    ).reshape(peers, gain_each, LANES)
    by_x = jnp.pad(bias_part.reshape(bias_lines, LANES), ((0, N_X * bias_each - bias_lines), (0, 0)))
    by_x = jnp.broadcast_to(by_x.reshape(N_X, 1, bias_each, LANES), (N_X, n_tensor, bias_each, LANES))
    lines = jnp.concatenate(
        [
            shared,
            by_x.reshape(peers, bias_each, LANES),
            jnp.zeros((peers, each - used, LANES), jnp.float32),
        ],
        1,
    )
    group = ("x", *TENSOR)
    column = lax.axis_index("zl") * N_C + core
    lines = lax.all_to_all(lines, group, 0, 0, tiled=True)
    line = lax.broadcasted_iota(jnp.int32, lines.shape, 1)
    sender = lax.broadcasted_iota(jnp.int32, lines.shape, 0) % n_tensor
    lines = jnp.sum(jnp.where((line < gain_each) | (sender == column), lines, 0.0), axis=0)
    lines = jnp.sum(spread(lines, "y", N_Y), axis=0)
    lines = jnp.sum(spread(lines, "zh", N_ZH), axis=0)
    lines = spread(lines, group, peers)
    shared = lines[:, :gain_each].reshape(peers * gain_each, LANES)
    gain_gradient_mean = shared[:gain_lines].reshape(width)
    distill_loss = shared[gain_lines, 0]
    by_x = lax.dynamic_slice_in_dim(
        lines[:, gain_each:used].reshape(N_X, n_tensor, bias_each, LANES), column, 1, 1
    )
    grad_bias = by_x.reshape(N_X * bias_each, LANES)[:bias_lines].reshape(columns)

    unscaled, inverse = normalized(hidden)
    for piece in pieces:
        portion_gradient = portion_gradient + piece.astype(jnp.float32)
    unscaled_gradient = portion_gradient * gain
    inner = jnp.mean(unscaled_gradient * unscaled, axis=-1, keepdims=True)
    hidden_gradient = (inverse * (unscaled_gradient - unscaled * inner)).astype(jnp.bfloat16)
    return (hidden_gradient, gain_gradient_mean, grad_bias, distill_loss)


def solution(mesh):
    split = Mesh(np.asarray(mesh.devices).reshape(SIZES), AXES)
    return jax.shard_map(
        shards,
        mesh=split,
        in_specs=(P(AXES, None), P(), P(DP, TENSOR), P(), P(), P(TENSOR), P(None, TENSOR)),
        out_specs=(P(AXES, None), P(), P(TENSOR), P()),
        check_vma=False,
    )
```

```python
import jax
import jax.numpy as jnp
import numpy as np
from jax import lax
from jax.sharding import Mesh, PartitionSpec as P


DOCS = 4
NORM_EPS = 1e-05

AXES = ("x", "y", "zh", "zl", "c")
SIZES = (4, 8, 4, 3, 2)
DP = ("x", "y", "zh")
TENSOR = ("zl", "c")
N_X, N_Y, N_ZH, N_ZL, N_C = SIZES
N_DP = N_X * N_Y * N_ZH
LANES = 128


def pull(value, steps):
    return lax.ppermute(value, DP, [((i + steps) % N_DP, i) for i in range(N_DP)])


def swap_cores(value):
    return lax.ppermute(value, "c", [(0, 1), (1, 0)])


def spread(value, axes, count):
    copies = lax.optimization_barrier(jnp.broadcast_to(value[None], (count, *value.shape)))
    return lax.all_to_all(copies, axes, 0, 0, tiled=True)


def own_first(value, core):
    parts = value.reshape(N_ZL, N_C, -1, *value.shape[1:])
    half = (value.shape[0] // N_C, *value.shape[1:])
    even, odd = parts[:, 0].reshape(half), parts[:, 1].reshape(half)
    first = core == 0
    return jnp.concatenate([jnp.where(first, even, odd), jnp.where(first, odd, even)], 0)


def normalized(rows):
    entries = rows.astype(jnp.float32)
    inverse = lax.rsqrt(jnp.mean(entries * entries, axis=-1, keepdims=True) + NORM_EPS)
    return entries * inverse, inverse


def shards(hidden, doc_ids, teacher, rotation, gain, bias, projection):
    core = lax.axis_index("c")
    here = (lax.axis_index("x") * N_Y + lax.axis_index("y")) * N_ZH + lax.axis_index("zh")
    turn = rotation[0] % N_DP
    portion_rows, width = hidden.shape
    block_rows = teacher.shape[0]
    columns = projection.shape[1]
    tokens = block_rows * N_DP
    features = columns * N_ZL * N_C

    gathered = spread(hidden, "zl", N_ZL)

    far = [lambda t, s=s: pull(t, s * N_ZH) if s else t for s in range(N_X * N_Y)]
    moved = lax.switch(turn // N_ZH, far, teacher)

    row_docs = lax.dynamic_slice_in_dim(doc_ids, here, 1, 0)[0]
    same_doc = jnp.sum((row_docs[:, None] == row_docs[None, :]).astype(jnp.float32), axis=-1)
    weight = own_first((block_rows / (DOCS * same_doc))[:, None], core)

    def near(step):
        def branch(t, mine, weight):
            target = pull(t, step) if step else t
            mine = mine.reshape(-1, width)
            other = swap_cores(mine)
            block = jnp.concatenate([mine, other], 0)
            unscaled, inverse = normalized(block)
            rows = (unscaled * gain).astype(jnp.bfloat16)
            logits = jnp.dot(rows, projection, preferred_element_type=jnp.float32) + bias
            logits = lax.optimization_barrier(logits)
            error = logits - own_first(target, core).astype(jnp.float32)
            loss_part = jnp.sum(weight * error * error) / (2.0 * tokens * features)
            grad_out = (weight * error).astype(jnp.bfloat16)
            bias_part = jnp.sum(grad_out.astype(jnp.float32), axis=0) / tokens
            grad_all = lax.dot_general(
                grad_out, projection, (((1,), (1,)), ((), ())), preferred_element_type=jnp.float32
            )
            return lax.optimization_barrier((grad_all, loss_part, bias_part, other, inverse))

        return branch

    grad_all, loss_part, bias_part, other, block_inverse = lax.switch(
        turn % N_ZH, [near(s) for s in range(N_ZH)], moved, gathered, weight
    )
    block = jnp.concatenate([gathered.reshape(-1, width), other], 0)
    gain_part = jnp.sum(grad_all * (block.astype(jnp.float32) * block_inverse), axis=0) / tokens
    half = block_rows // N_C
    own_rows = grad_all[:half]
    far_rows = grad_all[half:].astype(jnp.bfloat16)
    summed = own_rows + swap_cores(far_rows).astype(jnp.float32)
    summed = summed.reshape(N_ZL, portion_rows, width)
    at = lax.axis_index("zl")
    portion_gradient = lax.dynamic_index_in_dim(summed, at, 0, keepdims=False)
    pieces = []
    for step in range(1, N_ZL):
        piece = lax.dynamic_index_in_dim(summed, (at + step) % N_ZL, 0, keepdims=False)
        ring = [(i, (i + step) % N_ZL) for i in range(N_ZL)]
        pieces.append(lax.ppermute(piece.astype(jnp.bfloat16), "zl", ring))

    n_tensor = N_ZL * N_C
    peers = N_ZH * n_tensor
    gain_lines, bias_lines = width // LANES, columns // LANES
    gain_each, bias_each = -(-(gain_lines + 1) // peers), -(-bias_lines // N_ZH)
    used = gain_each + bias_each
    each = -(-used // 8) * 8
    shared = jnp.concatenate(
        [
            gain_part.reshape(gain_lines, LANES),
            jnp.broadcast_to(loss_part, (1, LANES)),
            jnp.zeros((peers * gain_each - gain_lines - 1, LANES), jnp.float32),
        ],
        0,
    ).reshape(peers, gain_each, LANES)
    by_zh = jnp.pad(bias_part.reshape(bias_lines, LANES), ((0, N_ZH * bias_each - bias_lines), (0, 0)))
    by_zh = jnp.broadcast_to(by_zh.reshape(N_ZH, 1, bias_each, LANES), (N_ZH, n_tensor, bias_each, LANES))
    lines = jnp.concatenate(
        [
            shared,
            by_zh.reshape(peers, bias_each, LANES),
            jnp.zeros((peers, each - used, LANES), jnp.float32),
        ],
        1,
    )
    group = ("zh", *TENSOR)
    column = lax.axis_index("zl") * N_C + core
    lines = lax.all_to_all(lines, group, 0, 0, tiled=True)
    line = lax.broadcasted_iota(jnp.int32, lines.shape, 1)
    sender = lax.broadcasted_iota(jnp.int32, lines.shape, 0) % n_tensor
    lines = jnp.sum(jnp.where((line < gain_each) | (sender == column), lines, 0.0), axis=0)
    lines = jnp.sum(spread(lines, ("x", "y"), N_X * N_Y), axis=0)
    lines = spread(lines, group, peers)
    shared = lines[:, :gain_each].reshape(peers * gain_each, LANES)
    gain_gradient_mean = shared[:gain_lines].reshape(width)
    distill_loss = shared[gain_lines, 0]
    by_zh = lax.dynamic_slice_in_dim(
        lines[:, gain_each:used].reshape(N_ZH, n_tensor, bias_each, LANES), column, 1, 1
    )
    grad_bias = by_zh.reshape(N_ZH * bias_each, LANES)[:bias_lines].reshape(columns)

    unscaled, inverse = normalized(hidden)
    for piece in pieces:
        portion_gradient = portion_gradient + piece.astype(jnp.float32)
    unscaled_gradient = portion_gradient * gain
    inner = jnp.mean(unscaled_gradient * unscaled, axis=-1, keepdims=True)
    hidden_gradient = (inverse * (unscaled_gradient - unscaled * inner)).astype(jnp.bfloat16)
    return (hidden_gradient, gain_gradient_mean, grad_bias, distill_loss)


def solution(mesh):
    split = Mesh(np.asarray(mesh.devices).reshape(SIZES), AXES)
    return jax.shard_map(
        shards,
        mesh=split,
        in_specs=(P(AXES, None), P(), P(DP, TENSOR), P(), P(), P(TENSOR), P(None, TENSOR)),
        out_specs=(P(AXES, None), P(), P(TENSOR), P()),
        check_vma=False,
    )
```
